32 devices in a mesh: row: 8 (over y, x, core), col: 4 (over z).
Axes of the slice: x: 2, y: 2, z: 4, core: 2. Of those that a mesh axis runs over, the one named last changes fastest.
Arguments:
- tracers: float32 [40, 6, 64, 512], P(None, None, 'row', 'col'), may hold values from 0.1 to 10
- wind: float32 [2, 6, 64, 512], P(None, None, 'row', 'col'), may hold values from -2.4 to 2.4
- bin_shift: int32 [64, 512], P('row', 'col'), may hold values from 0 to 3
- shift_frac: float32 [64, 512], P('row', 'col'), may hold values from 0 to 1
Outputs:
- aerosol: float32 [40, 6, 64, 512], P(None, None, 'row', 'col')
The draws below stay inside these ranges and needn't reach their ends.
All inputs are finite; a program needn't handle non-finite values.
Results may differ from the reference program's by a relative error of at most 0.0001.
Values sent between devices are 32-bit elements; how exact they have to be, the bound alone decides.
A program may use at most 64 MiB of HBM per device.

```python
import math
import jax
import jax.numpy as jnp
import numpy as np
from jax import lax

BINS = 40
LEV = 6
NR = 64
NC = 512


def set_ends(values, own_key, low, high):
    index_at = [jax.random.randint(jax.random.fold_in(own_key, axis), (), 0, length) for axis, length in enumerate(values.shape)]
    widest = values.shape.index(max(values.shape))
    next_to = index_at[:widest] + [(index_at[widest] + 1) % values.shape[widest]] + index_at[widest + 1:]
    return values.at[tuple(index_at)].set(low).at[tuple(next_to)].set(high)


def shard_levels(stream_key, shape, shards, least, top_value):
    loudness = 1.0
    for dim, blocks in shards:
        heights = jax.random.uniform(jax.random.fold_in(jax.random.fold_in(stream_key, 6), dim), (blocks,), jnp.float32, least / len(shards), top_value / len(shards))
        loudness = loudness * jnp.repeat(jnp.exp(heights), shape[dim] // blocks).reshape((-1,) + (1,) * (len(shape) - 1 - dim))
    return loudness


def scatter_about(stream_key, shape, deviation, limit, cuts=(), held_as=jnp.bfloat16):
    values = jax.random.normal(stream_key, shape, jnp.float32) * deviation
    if len(cuts) > 0:
        values = shard_levels(stream_key, shape, cuts, -0.22, 0.18) * values
    return jnp.clip(values, min=-limit, max=limit).astype(held_as)


def setup_inputs(seed: int = 0) -> dict:
    keys = jax.random.split(jax.random.key(seed), 5)
    return {
        "tracers": jnp.clip(jnp.exp(math.log(10.0) - 4.6051702 * jax.random.uniform(keys[0], (BINS, LEV, NR, NC), jnp.float32) ** shard_levels(keys[0], (BINS, LEV, NR, NC), ((2, 8), (3, 4)), -0.2, 0.2)), 0.1, 10.0),
        "wind": scatter_about(keys[1], (2, LEV, NR, NC), 0.4, 2.4, ((2, 8), (3, 4)), jnp.float32),
        "bin_shift": set_ends(jax.random.randint(keys[2], (NR, NC), 0, 4), jax.random.fold_in(keys[2], 1), 0, 3).astype(jnp.int32),
        "shift_frac": jnp.clip(1.0 * jax.random.uniform(keys[3], (NR, NC), jnp.float32) ** shard_levels(keys[3], (NR, NC), ((0, 8), (1, 4)), -0.2, 0.2), 0.0, 1.0),
    }


step_size = 0.25
hyper_coef = 0.001

def lobatto_derivative():
    points = np.array([-1.0, -1.0 / np.sqrt(5.0), 1.0 / np.sqrt(5.0), 1.0])
    weights = np.array([1.0 / np.prod([points[j] - points[k] for k in range(4) if k != j]) for j in range(4)])
    matrix = np.zeros((4, 4))
    for i in range(4):
        for j in range(4):
            if i != j:
                matrix[i, j] = weights[j] / weights[i] / (points[i] - points[j])
        matrix[i, i] = -np.sum(matrix[i])
    return matrix

def along_cols(field, deriv):
    shaped = field.reshape(field.shape[:-1] + (field.shape[-1] // 4, 4))
    result = jnp.einsum('...n,in->...i', shaped, deriv, precision=lax.Precision.HIGHEST)
    return result.reshape(field.shape)

def along_rows(field, deriv):
    return jnp.swapaxes(along_cols(jnp.swapaxes(field, -1, -2), deriv), -1, -2)

def seam_cols(field):
    shaped = field.reshape(field.shape[:-1] + (field.shape[-1] // 4, 4))
    merged = 0.5 * shaped[..., 3] + 0.5 * jnp.roll(shaped[..., 0], -1, axis=-1)
    shaped = shaped.at[..., 3].set(merged).at[..., 0].set(jnp.roll(merged, 1, axis=-1))
    return shaped.reshape(field.shape)

def assemble(field):
    rows_done = jnp.swapaxes(seam_cols(jnp.swapaxes(field, -1, -2)), -1, -2)
    return seam_cols(rows_done)

def tendency(field, wind_x, wind_y, deriv):
    slope_x = along_cols(field, deriv)
    slope_y = along_rows(field, deriv)
    laplace = along_cols(along_cols(field, deriv), deriv) + along_rows(along_rows(field, deriv), deriv)
    laplace = assemble(laplace)
    second = along_cols(along_cols(laplace, deriv), deriv) + along_rows(along_rows(laplace, deriv), deriv)
    return -(wind_x * slope_x + wind_y * slope_y) - hyper_coef * second

def shift_bins(field, amount):
    count = field.shape[0]
    pieces = [jnp.zeros((amount,) + field.shape[1:], field.dtype), field[:count - 1 - amount], lax.optimization_barrier(jnp.sum(field[count - 1 - amount:], axis=0, keepdims=True))]
    return jnp.concatenate(pieces, axis=0)

def remap(field, bin_shift, shift_frac):
    total = jnp.zeros_like(field)
    for amount in range(5):
        weight = jnp.where(bin_shift == amount, 1.0 - shift_frac, 0.0) + jnp.where(bin_shift + 1 == amount, shift_frac, 0.0)
        total = total + weight * shift_bins(field, amount)
    return total

def reference(tracers, wind, bin_shift, shift_frac):
    deriv = jnp.asarray(lobatto_derivative(), dtype=jnp.float32)

    def one_level(level):
        field = lax.dynamic_index_in_dim(tracers, level, 1, False)
        wind_x = lax.dynamic_index_in_dim(wind[0], level, 0, False)[None]
        wind_y = lax.dynamic_index_in_dim(wind[1], level, 0, False)[None]
        section_one = assemble(field + step_size * tendency(field, wind_x, wind_y, deriv))
        section_two = assemble(0.5 * field + 0.5 * (section_one + step_size * tendency(section_one, wind_x, wind_y, deriv)))
        return remap(section_two, bin_shift, shift_frac)
    levels = lax.map(one_level, jnp.arange(tracers.shape[1], dtype=jnp.int32))
    return jnp.moveaxis(levels, 0, 1)
```

```python
import functools
import jax
import jax.numpy as jnp
import numpy as np
from jax import lax
from jax.experimental import pallas as pl
from jax.experimental.pallas import tpu as pltpu
from jax.sharding import PartitionSpec as P

step_size = 0.25
hyper_coef = 0.001
MESH = pl.DeviceIdType.MESH
CHUNKS = 3
PHASES = 4
LEFT, RIGHT, UP_LEFT, UP_RIGHT, DOWN_LEFT, DOWN_RIGHT = range(6)


def lobatto_derivative():
    points = np.array([-1.0, -1.0 / np.sqrt(5.0), 1.0 / np.sqrt(5.0), 1.0])
    weights = np.array(
        [1.0 / np.prod([points[j] - points[k] for k in range(4) if k != j]) for j in range(4)]
    )
    matrix = np.zeros((4, 4))
    for i in range(4):
        for j in range(4):
            if i != j:
                matrix[i, j] = weights[j] / weights[i] / (points[i] - points[j])
        matrix[i, i] = -np.sum(matrix[i])
    return matrix


DERIV = lobatto_derivative()
SECOND = DERIV @ DERIV


def seam_table(length):
    table = np.zeros((length + 128, length))
    for node in range(length):
        place = node % 4
        if place == 1 or place == 2:
            table[node, node] = 1.0
            continue
        table[node, node] = 0.5
        other = node + 1 if place == 3 else node - 1
        if 0 <= other < length:
            table[other, node] = 0.5
    for lane in (LEFT, UP_LEFT, DOWN_LEFT):
        table[length + lane, 0] = 0.5
    for lane in (RIGHT, UP_RIGHT, DOWN_RIGHT):
        table[length + lane, length - 1] = 0.5
    return table


def tables(length):
    first = np.kron(np.eye(length // 4), DERIV.T)
    second = first @ first
    seam = seam_table(length)
    hyper = -step_size * hyper_coef
    made = (
        np.concatenate([-step_size * first, second], axis=1),
        np.concatenate([hyper * (seam @ second), seam], axis=1),
        np.concatenate([seam, -step_size * (seam @ first), seam @ second], axis=1),
        seam,
    )
    return [jnp.asarray(m, dtype=jnp.float32) for m in made]


def parts(f):
    s = [f[0] + f[3], f[1] + f[2]]
    return s[0] - s[1], f[0] - f[3], f[1] - f[2]


def first_rows(split, scale):
    m = DERIV * (0.5 * scale)
    ss, d0, d1 = split
    out = [None] * 4
    for i in range(2):
        odd = float(m[i, 0] + m[i, 3]) * ss
        even = float(m[i, 0] - m[i, 3]) * d0 + float(m[i, 1] - m[i, 2]) * d1
        out[i], out[3 - i] = even + odd, even - odd
    return out


def second_rows(split, scale):
    m = SECOND * (0.5 * scale)
    ss, d0, d1 = split
    out = [None] * 4
    for i in range(2):
        even = float(m[i, 0] + m[i, 3]) * ss
        odd = float(m[i, 0] - m[i, 3]) * d0 + float(m[i, 1] - m[i, 2]) * d1
        out[i], out[3 - i] = even + odd, even - odd
    return out


def by_elements(fn, rows):
    out = []
    for start in range(0, len(rows), 4):
        out += fn(parts(rows[start : start + 4]))
    return out


def transport(
    sizes, tr, wind, m0, m1, m2, m3, out, held, ahead, row_out, row_in, edge_out, edge_in,
    row_send, row_recv, edge_send, edge_recv,
):
    bins, levels, nr, nc = sizes
    step = levels // CHUNKS
    flat = step * nr * bins
    row_n, col_n = lax.axis_size("row"), lax.axis_size("col")
    row, col = lax.axis_index("row"), lax.axis_index("col")
    up, down = lax.rem(row + row_n - 1, row_n), lax.rem(row + 1, row_n)
    left, right = lax.rem(col + col_n - 1, col_n), lax.rem(col + 1, col_n)
    partners = [
        (up, col), (down, col), (row, left), (row, right),
        (up, left), (up, right), (down, left), (down, right),
    ]
    barrier = pltpu.get_barrier_semaphore()
    for partner in partners:
        pl.semaphore_signal(barrier, inc=1, device_id=partner, device_id_type=MESH)

    def copies(phase, chunk):
        slot = phase * CHUNKS + chunk
        made = []
        for side, partner in ((0, (up, col)), (1, (down, col))):
            made.append(pltpu.make_async_remote_copy(
                src_ref=row_out.at[slot, side], dst_ref=row_in.at[slot, 1 - side],
                send_sem=row_send.at[slot, side], recv_sem=row_recv.at[slot, 1 - side],
                device_id=partner, device_id_type=MESH,
            ))
        for side, lane, partner in (
            (0, RIGHT, (row, left)), (1, LEFT, (row, right)),
            (0, DOWN_RIGHT, (up, left)), (0, UP_RIGHT, (down, left)),
            (1, DOWN_LEFT, (up, right)), (1, UP_LEFT, (down, right)),
        ):
            made.append(pltpu.make_async_remote_copy(
                src_ref=edge_out.at[slot, side], dst_ref=edge_in.at[slot, lane],
                send_sem=edge_send.at[slot, lane], recv_sem=edge_recv.at[slot, lane],
                device_id=partner, device_id_type=MESH,
            ))
        return made

    def as_rows(field):
        shaped = field.reshape(step, nr, bins, nc)
        return [shaped[:, r] for r in range(nr)]

    def flatten(rows):
        return jnp.stack(rows, axis=1).reshape(flat, nc)

    def times(field, table):
        return jnp.dot(
            field, table[...], precision=lax.Precision.HIGHEST,
            preferred_element_type=jnp.float32,
        )

    def send(phase, chunk, rows):
        slot = phase * CHUNKS + chunk
        row_out[slot, 0] = rows[0]
        row_out[slot, 1] = rows[nr - 1]
        for r in range(nr):
            held[chunk, r] = rows[r]
        turned = flatten(rows).T
        edge_out[slot, 0] = turned[0:1]
        edge_out[slot, 1] = turned[nc - 1 : nc]
        if phase == 0 and chunk == 0:
            pl.semaphore_wait(barrier, len(partners))
        for copy in copies(phase, chunk):
            copy.start()

    def row_seam(rows, above, below):
        done = list(rows)
        for r in range(3, nr - 1, 4):
            done[r] = done[r + 1] = 0.5 * rows[r] + 0.5 * rows[r + 1]
        done[0] = 0.5 * rows[0] + 0.5 * above
        done[nr - 1] = 0.5 * rows[nr - 1] + 0.5 * below
        return done

    def joined(phase, chunk):
        slot = phase * CHUNKS + chunk
        for copy in copies(phase, chunk):
            copy.wait_recv()
        rows = row_seam([held[chunk, r] for r in range(nr)], row_in[slot, 0], row_in[slot, 1])
        lanes = jnp.concatenate(
            [edge_in[slot, i] for i in range(6)] + [jnp.zeros((122, flat), jnp.float32)], axis=0
        )
        edges = as_rows(lanes.T)
        lane = lax.broadcasted_iota(jnp.int32, edges[0].shape, 2)
        own = lane < 2
        side = [jnp.where(own, e, 0.0) for e in edges]
        from_up = jnp.where((lane >= 2) & (lane < 4), edges[nr - 1], 0.0)
        from_down = jnp.where((lane >= 4) & (lane < 6), edges[0], 0.0)
        side = row_seam(side, from_up, from_down)
        return jnp.concatenate([flatten(rows), flatten(side)], axis=1)

    def wind_rows(chunk, which):
        return [
            wind[which, chunk * step : (chunk + 1) * step, r : r + 1, :] for r in range(nr)
        ]

    def tracer_rows(chunk):
        rows = []
        for r in range(nr):
            pieces = [
                tr[pl.ds((chunk * step + l) * nr + r, bins, stride=levels * nr), :]
                for l in range(step)
            ]
            rows.append(jnp.stack(pieces, axis=0))
        return rows

    def lead(chunk, rows, slope_x, second_x, start, scale):
        wx, wy = wind_rows(chunk, 0), wind_rows(chunk, 1)
        slope_y = by_elements(lambda s: first_rows(s, -step_size), rows)
        second_y = by_elements(lambda s: second_rows(s, 1.0), rows)
        sx, lx = as_rows(slope_x), as_rows(second_x)
        laplace = []
        for r in range(nr):
            moved = rows[r] + wx[r] * sx[r] + wy[r] * slope_y[r]
            if start is not None:
                moved = scale * start[r] + scale * moved
            ahead[chunk, r] = moved
            laplace.append(lx[r] + second_y[r])
        return laplace

    def finish(chunk, made, scale):
        hx, h = as_rows(made[:, :nc]), as_rows(made[:, nc:])
        hy = by_elements(lambda s: second_rows(s, -step_size * hyper_coef), h)
        return [ahead[chunk, r] + scale * (hx[r] + hy[r]) for r in range(nr)]

    for chunk in range(CHUNKS):
        rows = tracer_rows(chunk)
        made = times(flatten(rows), m0)
        send(0, chunk, lead(chunk, rows, made[:, :nc], made[:, nc:], None, 1.0))
    for chunk in range(CHUNKS):
        send(1, chunk, finish(chunk, times(joined(0, chunk), m1), 1.0))
    for chunk in range(CHUNKS):
        made = times(joined(1, chunk), m2)
        rows = as_rows(made[:, :nc])
        send(2, chunk, lead(
            chunk, rows, made[:, nc : 2 * nc], made[:, 2 * nc :], tracer_rows(chunk), 0.5
        ))
    for chunk in range(CHUNKS):
        send(3, chunk, finish(chunk, times(joined(2, chunk), m1), 0.5))
    for chunk in range(CHUNKS):
        rows = as_rows(times(joined(3, chunk), m3))
        for r in range(nr):
            for l in range(step):
                out[pl.ds((chunk * step + l) * nr + r, bins, stride=levels * nr), :] = rows[r][l]
    for phase in range(PHASES):
        for chunk in range(CHUNKS):
            for copy in copies(phase, chunk):
                copy.wait_send()


def remap(sizes, field, shift, frac, out):
    bins, levels, nr, nc = sizes
    weights = []
    for amount in range(5):
        weights.append(
            jnp.where(shift[...] == amount, 1.0 - frac[...], 0.0)
            + jnp.where(shift[...] + 1 == amount, frac[...], 0.0)
        )
    for level in range(levels):
        for b in range(bins - 1):
            total = weights[0] * field[b, level]
            for k in range(1, min(b, 4) + 1):
                total = total + weights[k] * field[b - k, level]
            out[b, level] = total
        top = field[bins - 1, level]
        total = weights[0] * top
        for k in range(1, 5):
            top = top + field[bins - 1 - k, level]
            total = total + weights[k] * top
        out[bins - 1, level] = total


def body(tracers, wind, bin_shift, shift_frac):
    sizes = tracers.shape
    bins, levels, nr, nc = sizes
    step = levels // CHUNKS
    flat = step * nr * bins
    slots = PHASES * CHUNKS
    vmem = pl.BlockSpec(memory_space=pltpu.VMEM)
    field = pl.pallas_call(
        functools.partial(transport, sizes),
        out_shape=jax.ShapeDtypeStruct((bins * levels * nr, nc), jnp.float32),
        in_specs=[vmem] * 6,
        out_specs=vmem,
        scratch_shapes=[
            pltpu.VMEM((CHUNKS, nr, step, bins, nc), jnp.float32),
            pltpu.VMEM((CHUNKS, nr, step, bins, nc), jnp.float32),
            pltpu.VMEM((slots, 2, step, bins, nc), jnp.float32),
            pltpu.VMEM((slots, 2, step, bins, nc), jnp.float32),
            pltpu.VMEM((slots, 2, 1, flat), jnp.float32),
            pltpu.VMEM((slots, 6, 1, flat), jnp.float32),
            pltpu.SemaphoreType.DMA((slots, 2)),
            pltpu.SemaphoreType.DMA((slots, 2)),
            pltpu.SemaphoreType.DMA((slots, 6)),
            pltpu.SemaphoreType.DMA((slots, 6)),
        ],
        compiler_params=pltpu.CompilerParams(
            collective_id=0, has_side_effects=True, vmem_limit_bytes=40 << 20
        ),
        name="transport",
    )(tracers.reshape(bins * levels * nr, nc), wind, *tables(nc))
    return pl.pallas_call(
        functools.partial(remap, sizes),
        out_shape=jax.ShapeDtypeStruct(sizes, jnp.float32),
        in_specs=[vmem] * 3,
        out_specs=vmem,
        name="remap",
    )(field.reshape(sizes), bin_shift, shift_frac)


def solution(mesh):
    placed = (
        P(None, None, "row", "col"),
        P(None, None, "row", "col"),
        P("row", "col"),
        P("row", "col"),
    )
    return jax.shard_map(
        body, mesh=mesh, in_specs=placed, out_specs=P(None, None, "row", "col"), check_vma=False
    )
```

```python
import functools
import jax
import jax.numpy as jnp
import numpy as np
from jax import lax
from jax.experimental import pallas as pl
from jax.experimental.pallas import tpu as pltpu
from jax.sharding import PartitionSpec as P

step_size = 0.25
hyper_coef = 0.001
MESH = pl.DeviceIdType.MESH
CHUNKS = 2
PHASES = 4
COMM = True
LEFT, RIGHT, UP_LEFT, UP_RIGHT, DOWN_LEFT, DOWN_RIGHT = range(6)


def lobatto_derivative():
    points = np.array([-1.0, -1.0 / np.sqrt(5.0), 1.0 / np.sqrt(5.0), 1.0])
    weights = np.array(
        [1.0 / np.prod([points[j] - points[k] for k in range(4) if k != j]) for j in range(4)]
    )
    matrix = np.zeros((4, 4))
    for i in range(4):
        for j in range(4):
            if i != j:
                matrix[i, j] = weights[j] / weights[i] / (points[i] - points[j])
        matrix[i, i] = -np.sum(matrix[i])
    return matrix


DERIV = lobatto_derivative()
SECOND = DERIV @ DERIV


def seam_table(length):
    table = np.zeros((length + 128, length))
    for node in range(length):
        place = node % 4
        if place == 1 or place == 2:
            table[node, node] = 1.0
            continue
        table[node, node] = 0.5
        other = node + 1 if place == 3 else node - 1
        if 0 <= other < length:
            table[other, node] = 0.5
    for lane in (LEFT, UP_LEFT, DOWN_LEFT):
        table[length + lane, 0] = 0.5
    for lane in (RIGHT, UP_RIGHT, DOWN_RIGHT):
        table[length + lane, length - 1] = 0.5
    return table


def tables(length):
    first = np.kron(np.eye(length // 4), DERIV.T)
    second = first @ first
    seam = seam_table(length)
    hyper = -step_size * hyper_coef
    made = (
        np.concatenate([-step_size * first, second], axis=1),
        np.concatenate([hyper * (seam @ second), seam], axis=1),
        np.concatenate([-step_size * (seam @ first), seam @ second, seam], axis=1),
        seam,
    )
    return [m.astype(np.float32) for m in made]


def split_tables(length):
    high = [m.astype(jnp.bfloat16) for m in tables(length)]
    low = [
        (m - h.astype(np.float32)).astype(jnp.bfloat16) for m, h in zip(tables(length), high)
    ]
    opening = np.concatenate([high[0], low[0]], axis=1)
    rest = np.concatenate(
        [high[1], low[1][:, :length], high[2], low[2][:, : 2 * length], high[3]], axis=1
    )
    return [jnp.asarray(opening), jnp.asarray(rest)]


def parts(f):
    s = [f[0] + f[3], f[1] + f[2]]
    return s[0] - s[1], f[0] - f[3], f[1] - f[2]


def first_rows(split, scale):
    m = DERIV * (0.5 * scale)
    ss, d0, d1 = split
    out = [None] * 4
    for i in range(2):
        odd = float(m[i, 0] + m[i, 3]) * ss
        even = float(m[i, 0] - m[i, 3]) * d0 + float(m[i, 1] - m[i, 2]) * d1
        out[i], out[3 - i] = even + odd, even - odd
    return out


def second_rows(split, scale):
    m = SECOND * (0.5 * scale)
    ss, d0, d1 = split
    out = [None] * 4
    for i in range(2):
        even = float(m[i, 0] + m[i, 3]) * ss
        odd = float(m[i, 0] - m[i, 3]) * d0 + float(m[i, 1] - m[i, 2]) * d1
        out[i], out[3 - i] = even + odd, even - odd
    return out


def by_elements(fn, rows):
    out = []
    for start in range(0, len(rows), 4):
        out += fn(parts(rows[start : start + 4]))
    return out


def transport(
    sizes, tr_in, wind_in, shift_in, frac_in, opening_in, rest_in, out, field, wind, shift, frac,
    opening, rest, moved_on, held, ahead, row_out, row_in, edge_out, edge_in,
    row_send, row_recv, edge_send, edge_recv, tr_sem, in_sem,
):
    bins, levels, nr, nc = sizes
    step = levels // CHUNKS
    flat = step * nr * bins
    row_n, col_n = lax.axis_size("row"), lax.axis_size("col")
    row, col = lax.axis_index("row"), lax.axis_index("col")
    up, down = lax.rem(row + row_n - 1, row_n), lax.rem(row + 1, row_n)
    left, right = lax.rem(col + col_n - 1, col_n), lax.rem(col + 1, col_n)
    partners = [
        (up, col), (down, col), (row, left), (row, right),
        (up, left), (up, right), (down, left), (down, right),
    ]
    tr = field.reshape(bins * levels * nr, nc)
    tr_loads = []
    for chunk in range(CHUNKS):
        part = pl.ds(chunk * step, step)
        tr_loads.append(
            pltpu.make_async_copy(tr_in.at[:, part], field.at[:, part], tr_sem.at[chunk])
        )
    loads = [
        pltpu.make_async_copy(source, target, in_sem.at[i])
        for i, (source, target) in enumerate((
            (opening_in, opening), (wind_in, wind), (rest_in, rest), (shift_in, shift),
            (frac_in, frac),
        ))
    ]
    tr_loads[0].start()
    for load in loads[:2]:
        load.start()
    for load in tr_loads[1:] + loads[2:]:
        load.start()
    barrier = pltpu.get_barrier_semaphore()
    for partner in partners:
        pl.semaphore_signal(barrier, inc=1, device_id=partner, device_id_type=MESH)

    def copies(phase, chunk):
        slot = phase * CHUNKS + chunk
        made = []
        for side, partner in ((0, (up, col)), (1, (down, col))):
            made.append(pltpu.make_async_remote_copy(
                src_ref=row_out.at[slot, side], dst_ref=row_in.at[slot, 1 - side],
                send_sem=row_send.at[slot, side], recv_sem=row_recv.at[slot, 1 - side],
                device_id=partner, device_id_type=MESH,
            ))
        for side, lane, partner in (
            (0, RIGHT, (row, left)), (1, LEFT, (row, right)),
            (0, DOWN_RIGHT, (up, left)), (0, UP_RIGHT, (down, left)),
            (1, DOWN_LEFT, (up, right)), (1, UP_LEFT, (down, right)),
        ):
            made.append(pltpu.make_async_remote_copy(
                src_ref=edge_out.at[slot, side], dst_ref=edge_in.at[slot, lane],
                send_sem=edge_send.at[slot, lane], recv_sem=edge_recv.at[slot, lane],
                device_id=partner, device_id_type=MESH,
            ))
        return made

    def as_rows(field):
        shaped = field.reshape(step, nr, bins, nc)
        return [shaped[:, r] for r in range(nr)]

    def flatten(rows):
        return jnp.stack(rows, axis=1).reshape(flat, nc)

    def times(field, table, at, wide, low_at, low_wide):
        def dot(lhs, start, width):
            return jnp.dot(
                lhs, table[: lhs.shape[1], start : start + width],
                preferred_element_type=jnp.float32,
            )

        high = field.astype(jnp.bfloat16)
        low = (field - high.astype(jnp.float32)).astype(jnp.bfloat16)
        total = dot(high, at, wide) + dot(low, at, wide)
        cols = [total[:, i : i + nc] for i in range(0, wide, nc)]
        if low_wide:
            more = dot(high, low_at, low_wide)
            for i in range(low_wide // nc):
                cols[i] = cols[i] + more[:, i * nc : (i + 1) * nc]
        return [as_rows(c) for c in cols]

    def first_table(field):
        return times(field, opening, 0, 2 * nc, 2 * nc, 2 * nc)

    def hyper_table(field):
        return times(field, rest, 0, 2 * nc, 2 * nc, nc)

    def middle_table(field):
        return times(field, rest, 3 * nc, 3 * nc, 6 * nc, 2 * nc)

    def last_table(field):
        return times(field, rest, 8 * nc, nc, 0, 0)[0]

    def send(phase, chunk, rows):
        slot = phase * CHUNKS + chunk
        row_out[slot, 0] = rows[0]
        row_out[slot, 1] = rows[nr - 1]
        for r in range(nr):
            held[chunk, r] = rows[r]
        turned = flatten(rows).T
        edge_out[slot, 0] = turned[0:1]
        edge_out[slot, 1] = turned[nc - 1 : nc]
        if not COMM:
            return
        if phase == 0 and chunk == 0:
            pl.semaphore_wait(barrier, len(partners))
        for copy in copies(phase, chunk):
            copy.start()

    def row_seam(rows, above, below):
        done = list(rows)
        for r in range(3, nr - 1, 4):
            done[r] = done[r + 1] = 0.5 * rows[r] + 0.5 * rows[r + 1]
        done[0] = 0.5 * rows[0] + 0.5 * above
        done[nr - 1] = 0.5 * rows[nr - 1] + 0.5 * below
        return done

    def joined(phase, chunk):
        slot = phase * CHUNKS + chunk
        for copy in copies(phase, chunk) if COMM else ():
            copy.wait_recv()
        rows = row_seam([held[chunk, r] for r in range(nr)], row_in[slot, 0], row_in[slot, 1])
        lanes = jnp.concatenate(
            [edge_in[slot, i] for i in range(6)] + [jnp.zeros((122, flat), jnp.float32)], axis=0
        )
        edges = as_rows(lanes.T)
        lane = lax.broadcasted_iota(jnp.int32, edges[0].shape, 2)
        own = lane < 2
        side = [jnp.where(own, e, 0.0) for e in edges]
        from_up = jnp.where((lane >= 2) & (lane < 4), edges[nr - 1], 0.0)
        from_down = jnp.where((lane >= 4) & (lane < 6), edges[0], 0.0)
        side = row_seam(side, from_up, from_down)
        return jnp.concatenate([flatten(rows), flatten(side)], axis=1)

    def wind_rows(chunk, which):
        return [
            wind[which, chunk * step : (chunk + 1) * step, r : r + 1, :] for r in range(nr)
        ]

    def tracer_rows(chunk):
        rows = []
        for r in range(nr):
            pieces = [
                tr[pl.ds((chunk * step + l) * nr + r, bins, stride=levels * nr), :]
                for l in range(step)
            ]
            rows.append(jnp.stack(pieces, axis=0))
        return rows

    def lead(chunk, rows, slope_x, second_x, start, scale):
        wx, wy = wind_rows(chunk, 0), wind_rows(chunk, 1)
        slope_y = by_elements(lambda s: first_rows(s, -step_size), rows)
        second_y = by_elements(lambda s: second_rows(s, 1.0), rows)
        sx, lx = slope_x, second_x
        laplace = []
        for r in range(nr):
            moved = rows[r] + wx[r] * sx[r] + wy[r] * slope_y[r]
            if start is not None:
                moved = scale * start[r] + scale * moved
            ahead[chunk, r] = moved
            laplace.append(lx[r] + second_y[r])
        return laplace

    def finish(chunk, made, scale):
        hx, h = made
        hy = by_elements(lambda s: second_rows(s, -step_size * hyper_coef), h)
        return [ahead[chunk, r] + scale * (hx[r] + hy[r]) for r in range(nr)]

    def remap(weights, level):
        def at(b):
            return moved_on[(b * levels + level) * nr : (b * levels + level + 1) * nr, :]

        for b in range(bins - 1):
            total = weights[0] * at(b)
            for k in range(1, min(b, 4) + 1):
                total = total + weights[k] * at(b - k)
            out[b, level] = total
        top = at(bins - 1)
        total = weights[0] * top
        for k in range(1, 5):
            top = top + at(bins - 1 - k)
            total = total + weights[k] * top
        out[bins - 1, level] = total

    for chunk in range(CHUNKS):
        tr_loads[chunk].wait()
        if chunk == 0:
            loads[0].wait()
            loads[1].wait()
        rows = tracer_rows(chunk)
        send(0, chunk, lead(chunk, rows, *first_table(flatten(rows)), None, 1.0))
    for load in loads[2:]:
        load.wait()
    for chunk in range(CHUNKS):
        send(1, chunk, finish(chunk, hyper_table(joined(0, chunk)), 1.0))
    for chunk in range(CHUNKS):
        slope_x, second_x, rows = middle_table(joined(1, chunk))
        send(2, chunk, lead(chunk, rows, slope_x, second_x, tracer_rows(chunk), 0.5))
    for chunk in range(CHUNKS):
        send(3, chunk, finish(chunk, hyper_table(joined(2, chunk)), 0.5))
    weights = []
    for k in range(5):
        weights.append(
            jnp.where(shift[...] == k, 1.0 - frac[...], 0.0)
            + jnp.where(shift[...] + 1 == k, frac[...], 0.0)
        )
    for chunk in range(CHUNKS):
        rows = last_table(joined(3, chunk))
        for l in range(step):
            level = chunk * step + l
            for r in range(nr):
                moved_on[pl.ds(level * nr + r, bins, stride=levels * nr), :] = rows[r][l]
            remap(weights, level)
    for phase in range(PHASES if COMM else 0):
        for chunk in range(CHUNKS):
            for copy in copies(phase, chunk):
                copy.wait_send()


def body(tracers, wind, bin_shift, shift_frac):
    sizes = tracers.shape
    bins, levels, nr, nc = sizes
    step = levels // CHUNKS
    flat = step * nr * bins
    slots = PHASES * CHUNKS
    opening, rest = split_tables(nc)
    return pl.pallas_call(
        functools.partial(transport, sizes),
        out_shape=jax.ShapeDtypeStruct(sizes, jnp.float32),
        in_specs=[pl.BlockSpec(memory_space=pltpu.HBM)] * 6,
        out_specs=pl.BlockSpec(memory_space=pltpu.VMEM),
        scratch_shapes=[
            pltpu.VMEM(sizes, jnp.float32),
            pltpu.VMEM(wind.shape, jnp.float32),
            pltpu.VMEM(bin_shift.shape, jnp.int32),
            pltpu.VMEM(shift_frac.shape, jnp.float32),
            pltpu.VMEM(opening.shape, jnp.bfloat16),
            pltpu.VMEM(rest.shape, jnp.bfloat16),
            pltpu.VMEM((bins * levels * nr, nc), jnp.float32),
            pltpu.VMEM((CHUNKS, nr, step, bins, nc), jnp.float32),
            pltpu.VMEM((CHUNKS, nr, step, bins, nc), jnp.float32),
            pltpu.VMEM((slots, 2, step, bins, nc), jnp.float32),
            pltpu.VMEM((slots, 2, step, bins, nc), jnp.float32),
            pltpu.VMEM((slots, 2, 1, flat), jnp.float32),
            pltpu.VMEM((slots, 6, 1, flat), jnp.float32),
            pltpu.SemaphoreType.DMA((slots, 2)),
            pltpu.SemaphoreType.DMA((slots, 2)),
            pltpu.SemaphoreType.DMA((slots, 6)),
            pltpu.SemaphoreType.DMA((slots, 6)),
            pltpu.SemaphoreType.DMA((CHUNKS,)),
            pltpu.SemaphoreType.DMA((5,)),
        ],
        compiler_params=pltpu.CompilerParams(
            collective_id=0, has_side_effects=True, vmem_limit_bytes=63 << 20
        ),
        name="transport",
    )(tracers, wind, bin_shift, shift_frac, opening, rest)


def solution(mesh):
    placed = (
        P(None, None, "row", "col"),
        P(None, None, "row", "col"),
        P("row", "col"),
        P("row", "col"),
    )
    return jax.shard_map(
        body, mesh=mesh, in_specs=placed, out_specs=P(None, None, "row", "col"), check_vma=False
    )
```

```python
import functools
import jax
import jax.numpy as jnp
import numpy as np
from jax import lax
from jax.experimental import pallas as pl
from jax.experimental.pallas import tpu as pltpu
from jax.sharding import PartitionSpec as P

step_size = 0.25
hyper_coef = 0.001
MESH = pl.DeviceIdType.MESH
CHUNKS = 2
PHASES = 2
COMM = True
LEFT, RIGHT, UP_LEFT, UP_RIGHT, DOWN_LEFT, DOWN_RIGHT = range(6)


def lobatto_derivative():
    points = np.array([-1.0, -1.0 / np.sqrt(5.0), 1.0 / np.sqrt(5.0), 1.0])
    weights = np.array(
        [1.0 / np.prod([points[j] - points[k] for k in range(4) if k != j]) for j in range(4)]
    )
    matrix = np.zeros((4, 4))
    for i in range(4):
        for j in range(4):
            if i != j:
                matrix[i, j] = weights[j] / weights[i] / (points[i] - points[j])
        matrix[i, i] = -np.sum(matrix[i])
    return matrix


DERIV = lobatto_derivative()
SECOND = DERIV @ DERIV
HYPER = -step_size * hyper_coef


def seam_table(length):
    table = np.zeros((length + 128, length))
    for node in range(length):
        place = node % 4
        if place == 1 or place == 2:
            table[node, node] = 1.0
            continue
        table[node, node] = 0.5
        other = node + 1 if place == 3 else node - 1
        if 0 <= other < length:
            table[other, node] = 0.5
    for lane in (LEFT, UP_LEFT, DOWN_LEFT):
        table[length + lane, 0] = 0.5
    for lane in (RIGHT, UP_RIGHT, DOWN_RIGHT):
        table[length + lane, length - 1] = 0.5
    return table


def tables(length):
    first = np.kron(np.eye(length // 4), DERIV.T)
    second = first @ first
    seam = seam_table(length)
    inner = (seam @ second) @ seam[:length]
    inner[:, 0] += 0.5 * SECOND[3, 3] * seam[:, 0]
    inner[:, length - 1] += 0.5 * SECOND[0, 0] * seam[:, length - 1]
    last = np.concatenate([seam, HYPER * inner], axis=0)
    made = (
        np.concatenate([-step_size * first, second], axis=1),
        np.concatenate([-step_size * (last @ first), last @ second, last], axis=1),
    )
    return [m.astype(np.float32) for m in made]


def split_tables(length):
    high = [m.astype(jnp.bfloat16) for m in tables(length)]
    low = [
        (m - h.astype(np.float32)).astype(jnp.bfloat16) for m, h in zip(tables(length), high)
    ]
    opening = np.concatenate([high[0], low[0]], axis=1)
    rest = np.concatenate([high[1], low[1]], axis=1)
    return [jnp.asarray(opening), jnp.asarray(rest)]


def parts(f):
    s = [f[0] + f[3], f[1] + f[2]]
    return s[0] - s[1], f[0] - f[3], f[1] - f[2]


def first_rows(split, scale):
    m = DERIV * (0.5 * scale)
    ss, d0, d1 = split
    out = [None] * 4
    for i in range(2):
        odd = float(m[i, 0] + m[i, 3]) * ss
        even = float(m[i, 0] - m[i, 3]) * d0 + float(m[i, 1] - m[i, 2]) * d1
        out[i], out[3 - i] = even + odd, even - odd
    return out


def second_rows(split, scale):
    m = SECOND * (0.5 * scale)
    ss, d0, d1 = split
    out = [None] * 4
    for i in range(2):
        even = float(m[i, 0] + m[i, 3]) * ss
        odd = float(m[i, 0] - m[i, 3]) * d0 + float(m[i, 1] - m[i, 2]) * d1
        out[i], out[3 - i] = even + odd, even - odd
    return out


def by_elements(fn, rows):
    out = []
    for start in range(0, len(rows), 4):
        out += fn(parts(rows[start : start + 4]))
    return out


def outer_parts(base, lap):
    n = len(lap)
    m = [[float(HYPER * v) for v in line] for line in SECOND]
    first = base[0] + m[0][1] * lap[1] + m[0][2] * lap[2]
    first = first + (0.5 * m[0][3]) * (lap[3] + lap[4])
    final = base[n - 1] + m[3][2] * lap[n - 2] + m[3][1] * lap[n - 3]
    final = final + (0.5 * m[3][0]) * (lap[n - 4] + lap[n - 5])
    return first, final


def row_seam(rows, above, below):
    n = len(rows)
    done = list(rows)
    for r in range(3, n - 1, 4):
        done[r] = done[r + 1] = 0.5 * rows[r] + 0.5 * rows[r + 1]
    done[0] = 0.5 * rows[0] + 0.5 * above
    done[n - 1] = 0.5 * rows[n - 1] + 0.5 * below
    return done


def row_part(base, lap, above, below):
    n = len(lap)
    seamed = row_seam(lap, above[1], below[1])
    bent = by_elements(lambda s: second_rows(s, HYPER), seamed)
    ends = float(HYPER * SECOND[3, 3]), float(HYPER * SECOND[0, 0])
    joint = row_seam(
        [b + y for b, y in zip(base, bent)],
        above[0] + ends[0] * seamed[0], below[0] + ends[1] * seamed[n - 1],
    )
    return joint, seamed


def transport(
    sizes, tr_in, wind_in, shift_in, frac_in, opening_in, rest_in, out, field, wind, shift, frac,
    opening, rest, moved_on, held, held_lap, row_out, row_in, edge_out, edge_in,
    row_send, row_recv, edge_send, edge_recv, tr_sem, in_sem,
):
    bins, levels, nr, nc = sizes
    step = levels // CHUNKS
    flat = step * nr * bins
    row_n, col_n = lax.axis_size("row"), lax.axis_size("col")
    row, col = lax.axis_index("row"), lax.axis_index("col")
    up, down = lax.rem(row + row_n - 1, row_n), lax.rem(row + 1, row_n)
    left, right = lax.rem(col + col_n - 1, col_n), lax.rem(col + 1, col_n)
    partners = [
        (up, col), (down, col), (row, left), (row, right),
        (up, left), (up, right), (down, left), (down, right),
    ]
    tr = field.reshape(bins * levels * nr, nc)
    tr_loads = []
    for chunk in range(CHUNKS):
        part = pl.ds(chunk * step, step)
        tr_loads.append(
            pltpu.make_async_copy(tr_in.at[:, part], field.at[:, part], tr_sem.at[chunk])
        )
    loads = [
        pltpu.make_async_copy(source, target, in_sem.at[i])
        for i, (source, target) in enumerate((
            (opening_in, opening), (wind_in, wind), (rest_in, rest), (shift_in, shift),
            (frac_in, frac),
        ))
    ]
    tr_loads[0].start()
    for load in loads[:2]:
        load.start()
    for load in tr_loads[1:] + loads[2:]:
        load.start()
    barrier = pltpu.get_barrier_semaphore()
    for partner in partners:
        pl.semaphore_signal(barrier, inc=1, device_id=partner, device_id_type=MESH)

    def copies(phase, chunk):
        slot = phase * CHUNKS + chunk
        made = []
        for side, partner in ((0, (up, col)), (1, (down, col))):
            made.append(pltpu.make_async_remote_copy(
                src_ref=row_out.at[slot, side], dst_ref=row_in.at[slot, 1 - side],
                send_sem=row_send.at[slot, side], recv_sem=row_recv.at[slot, 1 - side],
                device_id=partner, device_id_type=MESH,
            ))
        for side, lane, partner in (
            (0, RIGHT, (row, left)), (1, LEFT, (row, right)),
            (0, DOWN_RIGHT, (up, left)), (0, UP_RIGHT, (down, left)),
            (1, DOWN_LEFT, (up, right)), (1, UP_LEFT, (down, right)),
        ):
            made.append(pltpu.make_async_remote_copy(
                src_ref=edge_out.at[slot, side], dst_ref=edge_in.at[slot, lane],
                send_sem=edge_send.at[slot, lane], recv_sem=edge_recv.at[slot, lane],
                device_id=partner, device_id_type=MESH,
            ))
        return made

    def as_rows(field):
        shaped = field.reshape(step, nr, bins, nc)
        return [shaped[:, r] for r in range(nr)]

    def flatten(rows):
        return jnp.stack(rows, axis=1).reshape(flat, nc)

    def times(field, table, at, wide, low_at, low_wide):
        def dot(lhs, start, width):
            return jnp.dot(
                lhs, table[: lhs.shape[1], start : start + width],
                preferred_element_type=jnp.float32,
            )

        high = field.astype(jnp.bfloat16)
        low = (field - high.astype(jnp.float32)).astype(jnp.bfloat16)
        total = dot(high, at, wide) + dot(low, at, wide)
        cols = [total[:, i : i + nc] for i in range(0, wide, nc)]
        if low_wide:
            more = dot(high, low_at, low_wide)
            for i in range(low_wide // nc):
                cols[i] = cols[i] + more[:, i * nc : (i + 1) * nc]
        return [as_rows(c) for c in cols]

    def first_table(field):
        return times(field, opening, 0, 2 * nc, 2 * nc, 2 * nc)

    def middle_table(field):
        return times(field, rest, 0, 3 * nc, 3 * nc, 3 * nc)

    def last_table(field):
        return times(field, rest, 2 * nc, nc, 5 * nc, nc)[0]

    def send(phase, chunk, base, lap):
        slot = phase * CHUNKS + chunk
        ends = outer_parts(base, lap)
        for side in range(2):
            row_out[slot, side, 0] = ends[side]
            row_out[slot, side, 1] = lap[side * (nr - 1)]
        base_t, lap_t = flatten(base).T, flatten(lap).T
        near = list(range(5)) + list(range(nc - 5, nc))
        lap_lines = [lap_t[i : i + 1] for i in near]
        base_lines = [base_t[i : i + 1] for i in near]
        ends = outer_parts(base_lines, lap_lines)
        for side in range(2):
            edge_out[slot, side, 0] = ends[side]
            edge_out[slot, side, 1] = lap_lines[side * (len(near) - 1)]
        if COMM:
            if phase == 0 and chunk == 0:
                pl.semaphore_wait(barrier, len(partners))
            for copy in copies(phase, chunk):
                copy.start()
        for r in range(nr):
            held[chunk, r] = base[r]
            held_lap[chunk, r] = lap[r]

    def joined(phase, chunk):
        slot = phase * CHUNKS + chunk
        for copy in copies(phase, chunk) if COMM else ():
            copy.wait_recv()
        rows, row_laps = row_part(
            [held[chunk, r] for r in range(nr)], [held_lap[chunk, r] for r in range(nr)],
            (row_in[slot, 0, 0], row_in[slot, 0, 1]), (row_in[slot, 1, 0], row_in[slot, 1, 1]),
        )

        def turned(kind):
            lines = [edge_in[slot, i, kind] for i in range(6)]
            blank = jnp.zeros((nc - 6, flat), jnp.float32)
            return as_rows(jnp.concatenate(lines + [blank], axis=0).T)

        base, lap = turned(0), turned(1)
        lane = lax.broadcasted_iota(jnp.int32, base[0].shape, 2)
        own, upper = lane < 2, (lane >= 2) & (lane < 4)
        lower = (lane >= 4) & (lane < 6)
        first, final = outer_parts(base, lap)

        def only(mask, value):
            return jnp.where(mask, value, 0.0)

        side, side_laps = row_part(
            [only(own, v) for v in base], [only(own, v) for v in lap],
            (only(upper, final), only(upper, lap[nr - 1])),
            (only(lower, first), only(lower, lap[0])),
        )
        return jnp.concatenate([flatten(v) for v in (rows, side, row_laps, side_laps)], axis=1)

    def wind_rows(chunk, which):
        return [
            wind[which, chunk * step : (chunk + 1) * step, r : r + 1, :] for r in range(nr)
        ]

    def tracer_rows(chunk):
        rows = []
        for r in range(nr):
            pieces = [
                tr[pl.ds((chunk * step + l) * nr + r, bins, stride=levels * nr), :]
                for l in range(step)
            ]
            rows.append(jnp.stack(pieces, axis=0))
        return rows

    def lead(chunk, rows, slope_x, second_x, start, scale):
        wx, wy = wind_rows(chunk, 0), wind_rows(chunk, 1)
        slope_y = by_elements(lambda s: first_rows(s, -step_size), rows)
        second_y = by_elements(lambda s: second_rows(s, 1.0), rows)
        sx, lx = slope_x, second_x
        base, lap = [], []
        for r in range(nr):
            moved = rows[r] + wx[r] * sx[r] + wy[r] * slope_y[r]
            bent = lx[r] + second_y[r]
            if start is not None:
                moved = scale * start[r] + scale * moved
                bent = scale * bent
            base.append(moved)
            lap.append(bent)
        return base, lap

    def remap(weights, level):
        def at(b):
            return moved_on[(b * levels + level) * nr : (b * levels + level + 1) * nr, :]

        for b in range(bins - 1):
            total = weights[0] * at(b)
            for k in range(1, min(b, 4) + 1):
                total = total + weights[k] * at(b - k)
            out[b, level] = total
        top = at(bins - 1)
        total = weights[0] * top
        for k in range(1, 5):
            top = top + at(bins - 1 - k)
            total = total + weights[k] * top
        out[bins - 1, level] = total

    for chunk in range(CHUNKS):
        tr_loads[chunk].wait()
        if chunk == 0:
            loads[0].wait()
            loads[1].wait()
        rows = tracer_rows(chunk)
        send(0, chunk, *lead(chunk, rows, *first_table(flatten(rows)), None, 1.0))
    for load in loads[2:]:
        load.wait()
    for chunk in range(CHUNKS):
        slope_x, second_x, rows = middle_table(joined(0, chunk))
        send(1, chunk, *lead(chunk, rows, slope_x, second_x, tracer_rows(chunk), 0.5))
    weights = []
    for k in range(5):
        weights.append(
            jnp.where(shift[...] == k, 1.0 - frac[...], 0.0)
            + jnp.where(shift[...] + 1 == k, frac[...], 0.0)
        )
    for chunk in range(CHUNKS):
        rows = last_table(joined(1, chunk))
        for l in range(step):
            level = chunk * step + l
            for r in range(nr):
                moved_on[pl.ds(level * nr + r, bins, stride=levels * nr), :] = rows[r][l]
            remap(weights, level)
    for phase in range(PHASES if COMM else 0):
        for chunk in range(CHUNKS):
            for copy in copies(phase, chunk):
                copy.wait_send()


def body(tracers, wind, bin_shift, shift_frac):
    sizes = tracers.shape
    bins, levels, nr, nc = sizes
    step = levels // CHUNKS
    flat = step * nr * bins
    slots = PHASES * CHUNKS
    opening, rest = split_tables(nc)
    return pl.pallas_call(
        functools.partial(transport, sizes),
        out_shape=jax.ShapeDtypeStruct(sizes, jnp.float32),
        in_specs=[pl.BlockSpec(memory_space=pltpu.HBM)] * 6,
        out_specs=pl.BlockSpec(memory_space=pltpu.VMEM),
        scratch_shapes=[
            pltpu.VMEM(sizes, jnp.float32),
            pltpu.VMEM(wind.shape, jnp.float32),
            pltpu.VMEM(bin_shift.shape, jnp.int32),
            pltpu.VMEM(shift_frac.shape, jnp.float32),
            pltpu.VMEM(opening.shape, jnp.bfloat16),
            pltpu.VMEM(rest.shape, jnp.bfloat16),
            pltpu.VMEM((bins * levels * nr, nc), jnp.float32),
            pltpu.VMEM((CHUNKS, nr, step, bins, nc), jnp.float32),
            pltpu.VMEM((CHUNKS, nr, step, bins, nc), jnp.float32),
            pltpu.VMEM((slots, 2, 2, step, bins, nc), jnp.float32),
            pltpu.VMEM((slots, 2, 2, step, bins, nc), jnp.float32),
            pltpu.VMEM((slots, 2, 2, 1, flat), jnp.float32),
            pltpu.VMEM((slots, 6, 2, 1, flat), jnp.float32),
            pltpu.SemaphoreType.DMA((slots, 2)),
            pltpu.SemaphoreType.DMA((slots, 2)),
            pltpu.SemaphoreType.DMA((slots, 6)),
            pltpu.SemaphoreType.DMA((slots, 6)),
            pltpu.SemaphoreType.DMA((CHUNKS,)),
            pltpu.SemaphoreType.DMA((5,)),
        ],
        compiler_params=pltpu.CompilerParams(
            collective_id=0, has_side_effects=True, vmem_limit_bytes=63 << 20
        ),
        name="transport",
    )(tracers, wind, bin_shift, shift_frac, opening, rest)


def solution(mesh):
    placed = (
        P(None, None, "row", "col"),
        P(None, None, "row", "col"),
        P("row", "col"),
        P("row", "col"),
    )
    return jax.shard_map(
        body, mesh=mesh, in_specs=placed, out_specs=P(None, None, "row", "col"), check_vma=False
    )
```

```python
import functools
import jax
import jax.numpy as jnp
import numpy as np
from jax import lax
from jax.experimental import pallas as pl
from jax.experimental.pallas import tpu as pltpu
from jax.sharding import PartitionSpec as P

step_size = 0.25
hyper_coef = 0.001
MESH = pl.DeviceIdType.MESH
CHUNKS = 3
PHASES = 2
COMM = True
LEFT, RIGHT, UP_LEFT, UP_RIGHT, DOWN_LEFT, DOWN_RIGHT = range(6)


def lobatto_derivative():
    points = np.array([-1.0, -1.0 / np.sqrt(5.0), 1.0 / np.sqrt(5.0), 1.0])
    weights = np.array(
        [1.0 / np.prod([points[j] - points[k] for k in range(4) if k != j]) for j in range(4)]
    )
    matrix = np.zeros((4, 4))
    for i in range(4):
        for j in range(4):
            if i != j:
                matrix[i, j] = weights[j] / weights[i] / (points[i] - points[j])
        matrix[i, i] = -np.sum(matrix[i])
    return matrix


DERIV = lobatto_derivative()
SECOND = DERIV @ DERIV
HYPER = -step_size * hyper_coef


def seam_table(length):
    table = np.zeros((length + 128, length))
    for node in range(length):
        place = node % 4
        if place == 1 or place == 2:
            table[node, node] = 1.0
            continue
        table[node, node] = 0.5
        other = node + 1 if place == 3 else node - 1
        if 0 <= other < length:
            table[other, node] = 0.5
    for lane in (LEFT, UP_LEFT, DOWN_LEFT):
        table[length + lane, 0] = 0.5
    for lane in (RIGHT, UP_RIGHT, DOWN_RIGHT):
        table[length + lane, length - 1] = 0.5
    return table


def tables(length):
    first = np.kron(np.eye(length // 4), DERIV.T)
    second = first @ first
    seam = seam_table(length)
    inner = (seam @ second) @ seam[:length]
    inner[:, 0] += 0.5 * SECOND[3, 3] * seam[:, 0]
    inner[:, length - 1] += 0.5 * SECOND[0, 0] * seam[:, length - 1]
    last = np.concatenate([seam, HYPER * inner], axis=0)
    made = (
        np.concatenate([-step_size * first, second], axis=1),
        np.concatenate([-step_size * (last @ first), last @ second, last], axis=1),
    )
    return [m.astype(np.float32) for m in made]


def split_tables(length):
    high = [m.astype(jnp.bfloat16) for m in tables(length)]
    low = [
        (m - h.astype(np.float32)).astype(jnp.bfloat16) for m, h in zip(tables(length), high)
    ]
    opening = np.concatenate([high[0], low[0]], axis=1)
    rest = np.concatenate([high[1], low[1]], axis=1)
    return [jnp.asarray(opening), jnp.asarray(rest)]


def parts(f):
    s = [f[0] + f[3], f[1] + f[2]]
    return s[0] - s[1], f[0] - f[3], f[1] - f[2]


def first_rows(split, scale):
    m = DERIV * (0.5 * scale)
    ss, d0, d1 = split
    out = [None] * 4
    for i in range(2):
        odd = float(m[i, 0] + m[i, 3]) * ss
        even = float(m[i, 0] - m[i, 3]) * d0 + float(m[i, 1] - m[i, 2]) * d1
        out[i], out[3 - i] = even + odd, even - odd
    return out


def second_rows(split, scale):
    m = SECOND * (0.5 * scale)
    ss, d0, d1 = split
    out = [None] * 4
    for i in range(2):
        even = float(m[i, 0] + m[i, 3]) * ss
        odd = float(m[i, 0] - m[i, 3]) * d0 + float(m[i, 1] - m[i, 2]) * d1
        out[i], out[3 - i] = even + odd, even - odd
    return out


def by_elements(fn, rows):
    out = []
    for start in range(0, len(rows), 4):
        out += fn(parts(rows[start : start + 4]))
    return out


def outer_parts(base, lap):
    n = len(lap)
    m = [[float(HYPER * v) for v in line] for line in SECOND]
    first = base[0] + m[0][1] * lap[1] + m[0][2] * lap[2]
    first = first + (0.5 * m[0][3]) * (lap[3] + lap[4])
    final = base[n - 1] + m[3][2] * lap[n - 2] + m[3][1] * lap[n - 3]
    final = final + (0.5 * m[3][0]) * (lap[n - 4] + lap[n - 5])
    return first, final


def row_seam(rows, above, below):
    n = len(rows)
    done = list(rows)
    for r in range(3, n - 1, 4):
        done[r] = done[r + 1] = 0.5 * rows[r] + 0.5 * rows[r + 1]
    done[0] = 0.5 * rows[0] + 0.5 * above
    done[n - 1] = 0.5 * rows[n - 1] + 0.5 * below
    return done


def row_part(base, lap, above, below):
    n = len(lap)
    seamed = row_seam(lap, above[1], below[1])
    bent = by_elements(lambda s: second_rows(s, HYPER), seamed)
    ends = float(HYPER * SECOND[3, 3]), float(HYPER * SECOND[0, 0])
    joint = row_seam(
        [b + y for b, y in zip(base, bent)],
        above[0] + ends[0] * seamed[0], below[0] + ends[1] * seamed[n - 1],
    )
    return joint, seamed


def transport(
    sizes, tr_in, wind_in, shift_in, frac_in, opening_in, rest_in, out, field, wind, shift, frac,
    opening, rest, moved_on, held, held_lap, row_out, row_in, edge_out, edge_in,
    row_send, row_recv, edge_send, edge_recv, tr_sem, in_sem,
):
    bins, levels, nr, nc = sizes
    step = levels // CHUNKS
    flat = step * nr * bins
    row_n, col_n = lax.axis_size("row"), lax.axis_size("col")
    row, col = lax.axis_index("row"), lax.axis_index("col")
    up, down = lax.rem(row + row_n - 1, row_n), lax.rem(row + 1, row_n)
    left, right = lax.rem(col + col_n - 1, col_n), lax.rem(col + 1, col_n)
    partners = [
        (up, col), (down, col), (row, left), (row, right),
        (up, left), (up, right), (down, left), (down, right),
    ]
    tr = field.reshape(bins * levels * nr, nc)
    tr_loads = []
    for chunk in range(CHUNKS):
        part = pl.ds(chunk * step, step)
        tr_loads.append(
            pltpu.make_async_copy(tr_in.at[:, part], field.at[:, part], tr_sem.at[chunk])
        )
    loads = [
        pltpu.make_async_copy(source, target, in_sem.at[i])
        for i, (source, target) in enumerate((
            (opening_in, opening), (wind_in, wind), (rest_in, rest), (shift_in, shift),
            (frac_in, frac),
        ))
    ]
    tr_loads[0].start()
    for load in loads[:2]:
        load.start()
    for load in tr_loads[1:] + loads[2:]:
        load.start()
    barrier = pltpu.get_barrier_semaphore()
    for partner in partners:
        pl.semaphore_signal(barrier, inc=1, device_id=partner, device_id_type=MESH)

    def copies(phase, chunk):
        slot = phase * CHUNKS + chunk
        made = []
        for side, partner in ((0, (up, col)), (1, (down, col))):
            made.append(pltpu.make_async_remote_copy(
                src_ref=row_out.at[slot, side], dst_ref=row_in.at[slot, 1 - side],
                send_sem=row_send.at[slot, side], recv_sem=row_recv.at[slot, 1 - side],
                device_id=partner, device_id_type=MESH,
            ))
        for side, lane, partner in (
            (0, RIGHT, (row, left)), (1, LEFT, (row, right)),
            (0, DOWN_RIGHT, (up, left)), (0, UP_RIGHT, (down, left)),
            (1, DOWN_LEFT, (up, right)), (1, UP_LEFT, (down, right)),
        ):
            made.append(pltpu.make_async_remote_copy(
                src_ref=edge_out.at[slot, side], dst_ref=edge_in.at[slot, lane],
                send_sem=edge_send.at[slot, lane], recv_sem=edge_recv.at[slot, lane],
                device_id=partner, device_id_type=MESH,
            ))
        return made

    def as_rows(field):
        shaped = field.reshape(step, nr, bins, nc)
        return [shaped[:, r] for r in range(nr)]

    def flatten(rows):
        return jnp.stack(rows, axis=1).reshape(flat, nc)

    def times(field, table, at, wide, low_at, low_wide):
        def dot(lhs, start, width):
            return jnp.dot(
                lhs, table[: lhs.shape[1], start : start + width],
                preferred_element_type=jnp.float32,
            )

        high = field.astype(jnp.bfloat16)
        low = (field - high.astype(jnp.float32)).astype(jnp.bfloat16)
        total = dot(high, at, wide) + dot(low, at, wide)
        cols = [total[:, i : i + nc] for i in range(0, wide, nc)]
        if low_wide:
            more = dot(high, low_at, low_wide)
            for i in range(low_wide // nc):
                cols[i] = cols[i] + more[:, i * nc : (i + 1) * nc]
        return [as_rows(c) for c in cols]

    def first_table(field):
        return times(field, opening, 0, 2 * nc, 2 * nc, 2 * nc)

    def middle_table(field):
        return times(field, rest, 0, 3 * nc, 3 * nc, 3 * nc)

    def last_table(field):
        return times(field, rest, 2 * nc, nc, 5 * nc, nc)[0]

    def send(phase, chunk, base, lap):
        slot = phase * CHUNKS + chunk
        ends = outer_parts(base, lap)
        for side in range(2):
            row_out[slot, side, 0] = ends[side]
            row_out[slot, side, 1] = lap[side * (nr - 1)]
        base_t, lap_t = flatten(base).T, flatten(lap).T
        near = list(range(5)) + list(range(nc - 5, nc))
        lap_lines = [lap_t[i : i + 1] for i in near]
        base_lines = [base_t[i : i + 1] for i in near]
        ends = outer_parts(base_lines, lap_lines)
        for side in range(2):
            edge_out[slot, side, 0] = ends[side]
            edge_out[slot, side, 1] = lap_lines[side * (len(near) - 1)]
        if COMM:
            if phase == 0 and chunk == 0:
                pl.semaphore_wait(barrier, len(partners))
            for copy in copies(phase, chunk):
                copy.start()
        for r in range(nr):
            held[chunk, r] = base[r]
            held_lap[chunk, r] = lap[r]

    def joined(phase, chunk):
        slot = phase * CHUNKS + chunk
        for copy in copies(phase, chunk) if COMM else ():
            copy.wait_recv()
        rows, row_laps = row_part(
            [held[chunk, r] for r in range(nr)], [held_lap[chunk, r] for r in range(nr)],
            (row_in[slot, 0, 0], row_in[slot, 0, 1]), (row_in[slot, 1, 0], row_in[slot, 1, 1]),
        )

        def turned(kind):
            lines = [edge_in[slot, i, kind] for i in range(6)]
            blank = jnp.zeros((nc - 6, flat), jnp.float32)
            return as_rows(jnp.concatenate(lines + [blank], axis=0).T)

        base, lap = turned(0), turned(1)
        lane = lax.broadcasted_iota(jnp.int32, base[0].shape, 2)
        own, upper = lane < 2, (lane >= 2) & (lane < 4)
        lower = (lane >= 4) & (lane < 6)
        first, final = outer_parts(base, lap)

        def only(mask, value):
            return jnp.where(mask, value, 0.0)

        side, side_laps = row_part(
            [only(own, v) for v in base], [only(own, v) for v in lap],
            (only(upper, final), only(upper, lap[nr - 1])),
            (only(lower, first), only(lower, lap[0])),
        )
        return jnp.concatenate([flatten(v) for v in (rows, side, row_laps, side_laps)], axis=1)

    def wind_rows(chunk, which):
        return [
            wind[which, chunk * step : (chunk + 1) * step, r : r + 1, :] for r in range(nr)
        ]

    def tracer_rows(chunk):
        rows = []
        for r in range(nr):
            pieces = [
                tr[pl.ds((chunk * step + l) * nr + r, bins, stride=levels * nr), :]
                for l in range(step)
            ]
            rows.append(jnp.stack(pieces, axis=0))
        return rows

    def lead(chunk, rows, slope_x, second_x, start, scale):
        wx, wy = wind_rows(chunk, 0), wind_rows(chunk, 1)
        slope_y = by_elements(lambda s: first_rows(s, -step_size), rows)
        second_y = by_elements(lambda s: second_rows(s, 1.0), rows)
        sx, lx = slope_x, second_x
        base, lap = [], []
        for r in range(nr):
            moved = rows[r] + wx[r] * sx[r] + wy[r] * slope_y[r]
            bent = lx[r] + second_y[r]
            if start is not None:
                moved = scale * start[r] + scale * moved
                bent = scale * bent
            base.append(moved)
            lap.append(bent)
        return base, lap

    def remap(weights, level):
        def at(b):
            return moved_on[(b * levels + level) * nr : (b * levels + level + 1) * nr, :]

        for b in range(bins - 1):
            total = weights[0] * at(b)
            for k in range(1, min(b, 4) + 1):
                total = total + weights[k] * at(b - k)
            out[b, level] = total
        top = at(bins - 1)
        total = weights[0] * top
        for k in range(1, 5):
            top = top + at(bins - 1 - k)
            total = total + weights[k] * top
        out[bins - 1, level] = total

    for chunk in range(CHUNKS):
        tr_loads[chunk].wait()
        if chunk == 0:
            loads[0].wait()
            loads[1].wait()
        rows = tracer_rows(chunk)
        send(0, chunk, *lead(chunk, rows, *first_table(flatten(rows)), None, 1.0))
    for load in loads[2:]:
        load.wait()
    for chunk in range(CHUNKS):
        slope_x, second_x, rows = middle_table(joined(0, chunk))
        send(1, chunk, *lead(chunk, rows, slope_x, second_x, tracer_rows(chunk), 0.5))
    weights = []
    for k in range(5):
        weights.append(
            jnp.where(shift[...] == k, 1.0 - frac[...], 0.0)
            + jnp.where(shift[...] + 1 == k, frac[...], 0.0)
        )
    for chunk in range(CHUNKS):
        rows = last_table(joined(1, chunk))
        for l in range(step):
            level = chunk * step + l
            for r in range(nr):
                moved_on[pl.ds(level * nr + r, bins, stride=levels * nr), :] = rows[r][l]
            remap(weights, level)
    for phase in range(PHASES if COMM else 0):
        for chunk in range(CHUNKS):
            for copy in copies(phase, chunk):
                copy.wait_send()


def body(tracers, wind, bin_shift, shift_frac):
    sizes = tracers.shape
    bins, levels, nr, nc = sizes
    step = levels // CHUNKS
    flat = step * nr * bins
    slots = PHASES * CHUNKS
    opening, rest = split_tables(nc)
    return pl.pallas_call(
        functools.partial(transport, sizes),
        out_shape=jax.ShapeDtypeStruct(sizes, jnp.float32),
        in_specs=[pl.BlockSpec(memory_space=pltpu.HBM)] * 6,
        out_specs=pl.BlockSpec(memory_space=pltpu.VMEM),
        scratch_shapes=[
            pltpu.VMEM(sizes, jnp.float32),
            pltpu.VMEM(wind.shape, jnp.float32),
            pltpu.VMEM(bin_shift.shape, jnp.int32),
            pltpu.VMEM(shift_frac.shape, jnp.float32),
            pltpu.VMEM(opening.shape, jnp.bfloat16),
            pltpu.VMEM(rest.shape, jnp.bfloat16),
            pltpu.VMEM((bins * levels * nr, nc), jnp.float32),
            pltpu.VMEM((CHUNKS, nr, step, bins, nc), jnp.float32),
            pltpu.VMEM((CHUNKS, nr, step, bins, nc), jnp.float32),
            pltpu.VMEM((slots, 2, 2, step, bins, nc), jnp.float32),
            pltpu.VMEM((slots, 2, 2, step, bins, nc), jnp.float32),
            pltpu.VMEM((slots, 2, 2, 1, flat), jnp.float32),
            pltpu.VMEM((slots, 6, 2, 1, flat), jnp.float32),
            pltpu.SemaphoreType.DMA((slots, 2)),
            pltpu.SemaphoreType.DMA((slots, 2)),
            pltpu.SemaphoreType.DMA((slots, 6)),
            pltpu.SemaphoreType.DMA((slots, 6)),
            pltpu.SemaphoreType.DMA((CHUNKS,)),
            pltpu.SemaphoreType.DMA((5,)),
        ],
        compiler_params=pltpu.CompilerParams(
            collective_id=0, has_side_effects=True, vmem_limit_bytes=63 << 20
        ),
        name="transport",
    )(tracers, wind, bin_shift, shift_frac, opening, rest)


def solution(mesh):
    placed = (
        P(None, None, "row", "col"),
        P(None, None, "row", "col"),
        P("row", "col"),
        P("row", "col"),
    )
    return jax.shard_map(
        body, mesh=mesh, in_specs=placed, out_specs=P(None, None, "row", "col"), check_vma=False
    )
```
